32 devices in a mesh: rows: 8 (over y, x, core), grp: 4 (over z).
Axes of the slice: x: 2, y: 2, z: 4, core: 2. Of those that a mesh axis runs over, the one named last changes fastest.
Arguments:
- residual_in: float32 [8192, 128], P(('rows', 'grp')), may hold values from -6 to 6
- solution_in: float32 [8192, 128], P(('rows', 'grp')), may hold values from -6 to 6
- descriptors: float32 [32, 8192], P(None, ('rows', 'grp')), may hold values from -6 to 6
- length_weights: float32 [32], replicated, may hold values from 0.015625 to 0.125
- amplitude: float32 [1], replicated, may hold values from 0.05 to 0.15
- noise: float32 [1], replicated, may hold values from 0.5 to 1.5
- block_inverse: float32 [2, 1024, 1024], P(None, 'grp'), may hold values from -2 to 2, as said below
- block_rows: int32 [2, 1024], replicated, may hold values from 0 to 8191, as said below
Outputs:
- solution_field: float32 [8192, 128], P(('rows', 'grp'))
- residual_field: float32 [8192, 128], P(('rows', 'grp'))
The draws below stay inside these ranges and needn't reach their ends.
Inputs may be any that keep to these rules, and one draw needn't show every extreme that they name: `block_rows`: for each step the 1024 rows are distinct; at most 128 of them lie in one device's rows (the rows of one index of rows+grp, 256 consecutive rows), and in every step some device holds exactly 128. `block_inverse`: each step's matrix is symmetric.
All inputs are finite; a program needn't handle non-finite values.
Results may differ from the reference program's by a relative error of at most 0.0001.
Values sent between devices are 32-bit elements; how exact they have to be, the bound alone decides.
No kernel may reach another device: no remote copies, remote signals or barrier semaphores. Data moves between devices by JAX's collectives and lax.ppermute only.
A program may use at most 64 MiB of HBM per device.

```python
import math
import jax
import jax.numpy as jnp
from jax import lax

DESC = 32
RHS = 128
ROWS_DEV = 256
BLOCK = 1024
STEPS = 2
MOST = 128
NTRAIN = 8192
DEVICES = 32


def draw_block_rows(key, part):

    def draw_step(step_key):
        key_full, key_perm, key_order, key_local = jax.random.split(step_key, 4)
        full_device = jax.random.randint(key_full, (), 0, DEVICES)
        slot_total = DEVICES * MOST
        shuffled = jax.random.permutation(key_perm, slot_total)
        slot_owner = shuffled // MOST
        counter = jnp.arange(slot_total, dtype=jnp.int32)
        priority = jnp.where(slot_owner == full_device, counter - slot_total, counter)
        chosen = shuffled[jnp.argsort(priority, stable=True)[:BLOCK]]
        chosen = jax.random.permutation(key_order, chosen)
        tables = jax.vmap(lambda subkey: jax.random.permutation(subkey, ROWS_DEV)[:MOST])(jax.random.split(key_local, DEVICES))
        owners = chosen // MOST
        return (owners * ROWS_DEV + tables[owners, chosen % MOST]).astype(jnp.int32)
    return jnp.stack([draw_step(jax.random.fold_in(key, 7 + step_index)) for step_index in range(STEPS)])


def draw_block_inverse(key, part):

    def draw_step(step_key):
        key_diag, key_off = jax.random.split(step_key)
        diagonal = jax.random.uniform(key_diag, (BLOCK,), jnp.float32, 0.5, 1.5)
        gauss = jax.random.normal(key_off, (BLOCK, BLOCK), jnp.float32) * (0.5 / BLOCK ** 0.5)
        symmetric = (gauss + gauss.T) * 0.5 ** 0.5
        symmetric = jnp.clip(symmetric, -0.5, 0.5)
        return symmetric + jnp.diag(diagonal)
    return jnp.stack([draw_step(jax.random.fold_in(key, 31 + step_index)) for step_index in range(STEPS)]).astype(jnp.float32)


def level_of(key, shape, cuts, smallest, top_value):
    loudness, own = 1.0, jax.random.fold_in(key, 6)
    for dim, shards_of in cuts:
        steps = jnp.exp(jax.random.uniform(jax.random.fold_in(own, dim), (shards_of,), jnp.float32, smallest / len(cuts), top_value / len(cuts)))
        loudness = loudness * jnp.repeat(steps, shape[dim] // shards_of).reshape([-1 if axis == dim else 1 for axis in range(len(shape))])
    return loudness


def gaussian(stream_key, extent, width, limit, pieces=(), kind=jnp.bfloat16):
    entries = jax.random.normal(stream_key, extent, jnp.float32) * width
    if len(pieces) > 0:
        entries = level_of(stream_key, extent, pieces, -0.22, 0.18) * entries
    return jnp.clip(entries, min=-limit, max=limit).astype(kind)


def setup_inputs(seed: int = 0) -> dict:
    seeds = jax.random.split(jax.random.key(seed), 9)
    residual_in = gaussian(seeds[0], (NTRAIN, RHS), 1.0, 6.0, ((0, 32),), jnp.float32)
    solution_in = gaussian(seeds[1], (NTRAIN, RHS), 1.0, 6.0, ((0, 32),), jnp.float32)
    descriptors = gaussian(seeds[2], (DESC, NTRAIN), 1.0, 6.0, ((1, 32),), jnp.float32)
    length_weights = jnp.clip(jnp.exp(jax.random.uniform(seeds[3], (DESC,), jnp.float32, math.log(0.015625), math.log(0.125))), 0.015625, 0.125)
    amplitude = jnp.clip(jax.random.uniform(seeds[4], (1,), jnp.float32, 0.05, 0.15), 0.05, 0.15)
    noise = jnp.clip(jax.random.uniform(seeds[5], (1,), jnp.float32, 0.5, 1.5), 0.5, 1.5)
    block_inverse = draw_block_inverse(jax.random.fold_in(seeds[8], 71), 0)
    block_rows = draw_block_rows(jax.random.fold_in(seeds[8], 71), 0)
    return dict(residual_in=residual_in, solution_in=solution_in, descriptors=descriptors, length_weights=length_weights, amplitude=amplitude, noise=noise, block_inverse=block_inverse, block_rows=block_rows)


def kernel_tile(points, others, weights, scale_value):
    weighted = points * weights[:, None]
    cross_terms = lax.dot_general(weighted, others, (((0,), (0,)), ((), ())), precision=lax.Precision.HIGHEST)
    own_sq = jnp.sum(weighted * points, axis=0)
    other_sq = jnp.sum(others * others * weights[:, None], axis=0)
    return scale_value * jnp.exp(-(own_sq[:, None] + other_sq[None, :] - 2.0 * cross_terms))


def reference(residual_in, solution_in, descriptors, length_weights, amplitude, noise, block_inverse, block_rows):
    residual = residual_in
    solution = solution_in
    shard_count = NTRAIN // ROWS_DEV
    for step_index in range(STEPS):
        rows_now = block_rows[step_index]
        block_res = residual[rows_now]
        block_points = descriptors[:, rows_now]
        update = jnp.dot(block_inverse[step_index], block_res, precision=lax.Precision.HIGHEST)
        stacked_res = residual.reshape(shard_count, ROWS_DEV, RHS)
        stacked_pts = descriptors.reshape(DESC, shard_count, ROWS_DEV).transpose(1, 0, 2)

        def shard_update(operands):
            res_part, pts_part = operands
            kernel_block = kernel_tile(pts_part, block_points, length_weights, amplitude[0])
            return res_part - jnp.dot(kernel_block, update, precision=lax.Precision.HIGHEST)

        residual = lax.map(shard_update, (stacked_res, stacked_pts)).reshape(NTRAIN, RHS)
        residual = residual.at[rows_now].add(-noise[0] * update)
        solution = solution.at[rows_now].add(update)
    return solution, residual
```

```python
import functools

import jax
import jax.numpy as jnp
from jax import lax
from jax.experimental import pallas as pl
from jax.experimental.pallas import tpu as pltpu
from jax.sharding import PartitionSpec as P


F32 = jnp.float32
BF16 = jnp.bfloat16
LANES = 128
VMEM = pl.BlockSpec(memory_space=pltpu.VMEM)
SMEM = pl.BlockSpec(memory_space=pltpu.SMEM)


def split2(x):
    hi = x.astype(BF16)
    return hi, (x - hi.astype(F32)).astype(BF16)


def split3(x):
    hi = x.astype(BF16)
    rest = x - hi.astype(F32)
    mid = rest.astype(BF16)
    return hi, mid, (rest - mid.astype(F32)).astype(BF16)


def mm(a, b):
    return lax.dot_general(a, b, (((1,), (0,)), ((), ())), preferred_element_type=F32)


def mm_nt(a, b):
    return lax.dot_general(a, b, (((1,), (1,)), ((), ())), preferred_element_type=F32)


def me(sizes):
    return lax.axis_index("rows"), lax.axis_index("grp")


def prep_kernel(sizes, b_ref, a_ref, st_ref, ah_ref, al_ref, a2_ref):
    rows_local, zsize, panel = sizes
    i, g = me(sizes)
    npos = b_ref.shape[1]
    for t in range(2):
        brow = b_ref[t : t + 1, :]
        hi, lo = split2(a_ref[t])
        both = jnp.concatenate([hi, lo], axis=0)
        if t == 1:
            a2_ref[...] = both
        for s in range(zsize):
            base = (i * zsize + jnp.bitwise_xor(g, s)) * rows_local
            row = lax.broadcasted_iota(jnp.int32, (rows_local, npos), 0)
            sel = jnp.where(row == brow - base, 1.0, 0.0).astype(BF16)
            span = slice(s * rows_local, (s + 1) * rows_local)
            st_ref[t, span, :] = sel
            out = mm_nt(both, sel).astype(BF16)
            ah_ref[t, :, span] = out[:panel]
            al_ref[t, :, span] = out[panel:]


def part_kernel(sizes, *refs):
    rows_local, zsize, panel, feats = sizes
    x_refs = refs[:zsize]
    st_ref, ah_ref, al_ref, send_ref, keep_ref, rr, dd = refs[zsize:]
    i, _ = me(sizes)
    core0 = (i % 2) == 0
    width = x_refs[0].shape[1]
    half = width // 2
    pieces = rows_local // LANES
    for s in range(zsize):
        hi, lo = split2(x_refs[s][:rows_local, :])
        rr[s * rows_local : (s + 1) * rows_local, :width] = hi
        rr[s * rows_local : (s + 1) * rows_local, width:] = lo
        for q in range(pieces):
            d3 = split3(x_refs[s][rows_local + q * feats : rows_local + (q + 1) * feats, :])
            at = s * rows_local + q * LANES
            for k in range(3):
                dd[k * feats : (k + 1) * feats, at : at + LANES] = d3[k]
    parts, points = [], []
    for t in range(2):
        wide = mm(ah_ref[t], rr[...])
        parts.append(wide[:, :width] + wide[:, width:] + mm(al_ref[t], rr[:, :width]))
        three = mm(dd[...], st_ref[t])
        points.append(three[:feats] + three[feats : 2 * feats] + three[2 * feats :])
    low = jnp.concatenate([parts[0][:, :half], parts[1][:, :half]], axis=1)
    high = jnp.concatenate([parts[0][:, half:], parts[1][:, half:]], axis=1)
    keep_ref[:panel, :] = jnp.where(core0, low, high)
    send_ref[:panel, :] = jnp.where(core0, high, low)
    npos = points[0].shape[1]
    for q in range(npos // LANES):
        at = panel + q * feats
        first = points[0][:, q * LANES : (q + 1) * LANES]
        second = points[1][:, q * LANES : (q + 1) * LANES]
        keep_ref[at : at + feats, :] = jnp.where(core0, first, second)
        send_ref[at : at + feats, :] = jnp.where(core0, second, first)


def add_kernel(a_ref, b_ref, o_ref):
    o_ref[...] = a_ref[...] + b_ref[...]


def total_kernel(panel, count, *refs):
    pts_ref, u_ref, v_ref = refs[count:]
    total = refs[0][...]
    for k in range(1, count):
        total = total + refs[k][...]
    pts_ref[...] = total[panel:, :]
    half = total.shape[1] // 2
    u = total[:panel, :half]
    v = total[:panel, half:]
    u_ref[...] = jnp.concatenate([u[: panel // 2], u[panel // 2 :]], axis=1)
    v_ref[...] = jnp.concatenate([v[: panel // 2], v[panel // 2 :]], axis=1)


def features(x, w_col, left):
    weighted = x * w_col
    sq = jnp.sum(weighted * x, axis=0, keepdims=True)
    n = x.shape[1]
    row = lax.broadcasted_iota(jnp.int32, (16, n), 0)
    s0, s1, s2 = (p.astype(F32) for p in split3(sq))
    one = jnp.ones((1, n), F32)
    if left:
        a, b, c = split3(2.0 * weighted)
        extra = jnp.where(row == 0, s0, jnp.where(row == 1, s1, jnp.where(row == 2, s2, 0.0)))
        extra = jnp.where((row >= 3) & (row < 6), 1.0, extra)
        order = (a, a, b, b, a, c)
    else:
        a, b, c = split3(x)
        extra = jnp.where(row == 3, -s0, jnp.where(row == 4, -s1, jnp.where(row == 5, -s2, 0.0)))
        extra = jnp.where(row < 3, -1.0, extra)
        order = (a, b, a, b, c, a)
    return jnp.concatenate(list(order) + [extra.astype(BF16)], axis=0)


def tile_kernel(sizes, own_ref, oth_ref, d_ref, w_ref, b_ref, s_ref, kh_ref, kl_ref, o1h_ref, o1l_ref, o2h_ref, o2l_ref):
    feats, npos = sizes
    i, _ = me(sizes)
    core0 = (i % 2) == 0
    amp, noise = s_ref[0], s_ref[1]
    w_col = w_ref[...]
    own = jnp.concatenate([own_ref[q * feats : (q + 1) * feats, :] for q in range(npos // LANES)], axis=1)
    oth = jnp.concatenate([oth_ref[q * feats : (q + 1) * feats, :] for q in range(npos // LANES)], axis=1)
    x1 = jnp.where(core0, own, oth)
    x2 = jnp.where(core0, oth, own)
    right1 = features(x1, w_col, False)
    right2 = features(x2, w_col, False)
    mine = features(d_ref[...], w_col, True).astype(F32).T.astype(BF16)
    for right, h_ref, l_ref in ((right1, o1h_ref, o1l_ref), (right2, o2h_ref, o2l_ref)):
        hi, lo = split2(amp * jnp.exp(mm(mine, right)))
        h_ref[...] = hi
        l_ref[...] = lo
    left2 = features(x2, w_col, True).astype(F32).T.astype(BF16)
    b1 = b_ref[0:1, :]
    step = 128
    for r in range(npos // step):
        rows = slice(r * step, (r + 1) * step)
        b2 = jnp.broadcast_to(b_ref[1:2, rows], (step, step)).T[:, :1]
        tile = amp * jnp.exp(mm(left2[rows], right1)) + jnp.where(b2 == b1, noise, 0.0)
        hi, lo = split2(tile)
        kh_ref[rows, :] = hi
        kl_ref[rows, :] = lo


def solve_kernel(sizes, *refs):
    zsize, panel, half = sizes
    u_refs = refs[:zsize]
    v_ref, kh_ref, kl_ref, a2_ref, o_ref, uu = refs[zsize:]
    _, g = me(sizes)
    for s in range(zsize):
        x = u_refs[s][...]
        x = jnp.concatenate([x[:, :half], x[:, half:]], axis=0)
        hi, lo = split2(x)
        at = pl.multiple_of(jnp.bitwise_xor(g, s) * panel, panel)
        uu[pl.ds(at, panel), :] = jnp.concatenate([hi, lo], axis=1)
    y = mm(kh_ref[...], uu[...])
    w = y[:, :half] + y[:, half:] + mm(kl_ref[...], uu[...])[:, :half]
    hi, lo = split2(w)
    y = mm(a2_ref[...], jnp.concatenate([hi, lo], axis=1))
    y = y[:panel, :half] + y[:panel, half:] + y[panel:, :half]
    o_ref[...] = v_ref[...] - jnp.concatenate([y[: panel // 2], y[panel // 2 :]], axis=1)


def apply_kernel(sizes, r_ref, x_ref, kh_ref, kl_ref, st_ref, own_ref, oth_ref, s_ref, ro_ref, xo_ref, uu):
    zsize, panel, half = sizes
    i, g = me(sizes)
    core0 = (i % 2) == 0
    noise = s_ref[1]
    width = 2 * half
    hp = panel // 2
    for s in range(zsize):
        own = own_ref[s * hp : (s + 1) * hp, :]
        oth = oth_ref[s * hp : (s + 1) * hp, :]
        low = jnp.where(core0, own, oth)
        high = jnp.where(core0, oth, own)
        x = jnp.concatenate(
            [
                jnp.concatenate([low[:, :half], high[:, :half]], axis=1),
                jnp.concatenate([low[:, half:], high[:, half:]], axis=1),
            ],
            axis=0,
        )
        hi, lo = split2(x)
        at = pl.multiple_of(jnp.bitwise_xor(g, s) * panel, panel)
        uu[pl.ds(at, panel), :] = jnp.concatenate([hi, lo], axis=1)
    u = uu[...]
    wide = mm(kh_ref[...], u)
    kernel_sum = wide[:, :width] + wide[:, width:] + mm(kl_ref[...], u[:, :width])
    wide = mm(st_ref[...], u)
    inc = wide[:, :width] + wide[:, width:]
    ro_ref[...] = r_ref[...] - kernel_sum - noise * inc
    xo_ref[...] = x_ref[...] + inc


def call(kernel, out_shape, n_in, flops, nbytes, scratch=(), smem_at=(), aliases=None):
    specs = [SMEM if k in smem_at else VMEM for k in range(n_in)]
    return pl.pallas_call(
        kernel,
        out_shape=out_shape,
        in_specs=specs,
        out_specs=jax.tree.map(lambda _: VMEM, out_shape),
        scratch_shapes=list(scratch),
        compiler_params=pltpu.CompilerParams(vmem_limit_bytes=40 << 20),
        cost_estimate=pl.CostEstimate(flops=flops, bytes_accessed=nbytes, transcendentals=0),
    )


def sds(shape, dtype):
    return jax.ShapeDtypeStruct(shape, dtype)


def local(residual_in, solution_in, descriptors, length_weights, amplitude, noise, block_inverse, block_rows):
    rows_local, width = residual_in.shape
    feats = descriptors.shape[0]
    steps, npos = block_rows.shape
    assert steps == 2
    zsize, rsize = lax.axis_size("grp"), lax.axis_size("rows")
    panel = npos // zsize
    half = width // 2
    line = zsize * rows_local
    pts_rows = feats * npos // LANES

    def over_z(x, s):
        return lax.ppermute(x, "grp", [(k, k ^ s) for k in range(zsize)])

    def over_rows(x, s):
        return lax.ppermute(x, "rows", [(k, k ^ s) for k in range(rsize)])

    scalars = jnp.concatenate([amplitude, noise])
    pieces = [descriptors[:, q * LANES : (q + 1) * LANES] for q in range(rows_local // LANES)]
    packed = jnp.concatenate([residual_in] + pieces, axis=0)
    raw = [packed] + [over_z(packed, s) for s in range(1, zsize)]

    st, ah, al, a2 = call(
        functools.partial(prep_kernel, (rows_local, zsize, panel)),
        (
            sds((2, line, npos), BF16),
            sds((2, panel, line), BF16),
            sds((2, panel, line), BF16),
            sds((2 * panel, npos), BF16),
        ),
        2,
        4 * 2 * panel * line * npos,
        12 << 20,
    )(block_rows, block_inverse)

    send, keep = call(
        functools.partial(part_kernel, (rows_local, zsize, panel, feats)),
        (sds((panel + pts_rows, width), F32),) * 2,
        zsize + 3,
        2 * 2 * panel * line * width * 3,
        8 << 20,
        scratch=[pltpu.VMEM((line, 2 * width), BF16), pltpu.VMEM((3 * feats, line), BF16)],
    )(*raw, st, ah, al)

    got = over_rows(send, 1)
    pair = call(add_kernel, sds(keep.shape, F32), 2, keep.size, 12 * keep.size)(keep, got)
    plane = [pair] + [over_rows(pair, s) for s in range(2, rsize, 2)]
    points, u1, v2 = call(
        functools.partial(total_kernel, panel, len(plane)),
        (sds((pts_rows, width), F32), sds((panel // 2, width), F32), sds((panel // 2, width), F32)),
        len(plane),
        keep.size * len(plane),
        4 * keep.size * len(plane),
    )(*plane)

    points_oth = over_rows(points, 1)
    u1_all = [u1] + [over_z(u1, s) for s in range(1, zsize)]

    kh, kl, o1h, o1l, o2h, o2l = call(
        functools.partial(tile_kernel, (feats, npos)),
        (sds((npos, npos), BF16),) * 2 + (sds((rows_local, npos), BF16),) * 4,
        6,
        2 * npos * npos * 256,
        8 << 20,
        smem_at=(5,),
    )(points, points_oth, descriptors, length_weights[:, None], block_rows, scalars)

    u2 = call(
        functools.partial(solve_kernel, (zsize, panel, half)),
        sds((panel // 2, width), F32),
        zsize + 4,
        2 * npos * npos * width * 2,
        6 << 20,
        scratch=[pltpu.VMEM((npos, width), BF16)],
    )(*u1_all, v2, kh, kl, a2)
    u2_all = [u2] + [over_z(u2, s) for s in range(1, zsize)]

    finish = call(
        functools.partial(apply_kernel, (zsize, panel, half)),
        (sds(residual_in.shape, F32),) * 2,
        8,
        2 * rows_local * npos * width * 5,
        4 << 20,
        scratch=[pltpu.VMEM((npos, 2 * width), BF16)],
        smem_at=(7,),
    )
    own1 = jnp.concatenate(u1_all, axis=0)
    oth1 = over_rows(own1, 1)
    residual, sol = finish(residual_in, solution_in, o1h, o1l, st[0, :rows_local], own1, oth1, scalars)
    own2 = jnp.concatenate(u2_all, axis=0)
    oth2 = over_rows(own2, 1)
    residual, sol = finish(residual, sol, o2h, o2l, st[1, :rows_local], own2, oth2, scalars)
    return sol, residual


def solution(mesh):
    both = P(("rows", "grp"), None)
    return jax.shard_map(
        local,
        mesh=mesh,
        in_specs=(both, both, P(None, ("rows", "grp")), P(), P(), P(), P(None, "grp", None), P()),
        out_specs=(both, both),
        check_vma=False,
    )
```

```python
import functools

import jax
import jax.numpy as jnp
from jax import lax
from jax.experimental import pallas as pl
from jax.experimental.pallas import tpu as pltpu
from jax.sharding import PartitionSpec as P


F32 = jnp.float32
BF16 = jnp.bfloat16
VMEM = pl.BlockSpec(memory_space=pltpu.VMEM)
SMEM = pl.BlockSpec(memory_space=pltpu.SMEM)


def split2(x):
    hi = x.astype(BF16)
    return hi, (x - hi.astype(F32)).astype(BF16)


def split3(x):
    hi = x.astype(BF16)
    rest = x - hi.astype(F32)
    mid = rest.astype(BF16)
    return hi, mid, (rest - mid.astype(F32)).astype(BF16)


def mm(a, b):
    return lax.dot_general(a, b, (((1,), (0,)), ((), ())), preferred_element_type=F32)


def mm_nt(a, b):
    return lax.dot_general(a, b, (((1,), (1,)), ((), ())), preferred_element_type=F32)


def me():
    return lax.axis_index("rows"), lax.axis_index("grp")


def select_kernel(sizes, b_ref, st_ref, own1_ref, own2_ref):
    rows_local, zsize = sizes
    i, g = me()
    npos = b_ref.shape[1]
    row = lax.broadcasted_iota(jnp.int32, (rows_local, npos), 0)
    for t in range(2):
        for s in range(zsize):
            base = (i * zsize + jnp.bitwise_xor(g, s)) * rows_local
            sel = jnp.where(row == b_ref[t : t + 1, :] - base, 1.0, 0.0).astype(BF16)
            st_ref[t, s * rows_local : (s + 1) * rows_local, :] = sel
            if s == 0:
                (own1_ref, own2_ref)[t][...] = sel


def columns_kernel(sizes, a_ref, st_ref, ah_ref, al_ref, a2_ref):
    panel = sizes
    for t in range(2):
        hi, lo = split2(a_ref[t])
        both = jnp.concatenate([hi, lo], axis=0)
        if t == 1:
            a2_ref[...] = both
        out = mm_nt(both, st_ref[t]).astype(BF16)
        ah_ref[t] = out[:panel]
        al_ref[t] = out[panel:]


def points_kernel(sizes, *refs):
    _, zsize, feats = sizes
    d_refs = refs[:zsize]
    st_ref, send_ref, keep_ref = refs[zsize:]
    i, _ = me()
    core0 = (i % 2) == 0
    d = jnp.concatenate([r[...] for r in d_refs], axis=1)
    d3 = jnp.concatenate(list(split3(d)), axis=0)
    points = []
    for t in range(2):
        three = mm(d3, st_ref[t])
        points.append(three[:feats] + three[feats : 2 * feats] + three[2 * feats :])
    keep_ref[...] = jnp.where(core0, points[0], points[1])
    send_ref[...] = jnp.where(core0, points[1], points[0])


def fold(x):
    n = x.shape[0] // 2
    return jnp.concatenate([x[:n], x[n:]], axis=1)


def part_kernel(sizes, *refs):
    rows_local, zsize, panel = sizes
    x_refs = refs[:zsize]
    ah_ref, al_ref, send_ref, keep_ref, rr = refs[zsize:]
    i, _ = me()
    core0 = (i % 2) == 0
    width = x_refs[0].shape[1]
    half = width // 2
    hp = panel // 2
    for s in range(zsize):
        hi, lo = split2(x_refs[s][...])
        rr[s * rows_local : (s + 1) * rows_local, :width] = hi
        rr[s * rows_local : (s + 1) * rows_local, width:] = lo
    for t in range(2):
        wide = mm(ah_ref[t], rr[...])
        part = wide[:, :width] + wide[:, width:] + mm(al_ref[t], rr[:, :width])
        low, high = fold(part[:, :half]), fold(part[:, half:])
        keep_ref[t * hp : (t + 1) * hp, :] = jnp.where(core0, low, high)
        send_ref[t * hp : (t + 1) * hp, :] = jnp.where(core0, high, low)


def add_kernel(a_ref, b_ref, o_ref):
    o_ref[...] = a_ref[...] + b_ref[...]


def pair_kernel(a_ref, b_ref, u_ref, v_ref):
    n = u_ref.shape[0]
    u_ref[...] = a_ref[:n, :] + b_ref[:n, :]
    v_ref[...] = a_ref[n:, :] + b_ref[n:, :]


def sum_kernel(*refs):
    total = refs[0][...]
    for r in refs[1:-1]:
        total = total + r[...]
    refs[-1][...] = total


def features(x, w_col, left):
    weighted = x * w_col
    sq = jnp.sum(weighted * x, axis=0, keepdims=True)
    n = x.shape[1]
    row = lax.broadcasted_iota(jnp.int32, (16, n), 0)
    s0, s1, s2 = (p.astype(F32) for p in split3(sq))
    one = jnp.ones((1, n), F32)
    if left:
        a, b, c = split3(2.0 * weighted)
        extra = jnp.where(row == 0, s0, jnp.where(row == 1, s1, jnp.where(row == 2, s2, 0.0)))
        extra = jnp.where((row >= 3) & (row < 6), 1.0, extra)
        order = (a, a, b, b, a, c)
    else:
        a, b, c = split3(x)
        extra = jnp.where(row == 3, -s0, jnp.where(row == 4, -s1, jnp.where(row == 5, -s2, 0.0)))
        extra = jnp.where(row < 3, -1.0, extra)
        order = (a, b, a, b, c, a)
    return jnp.concatenate(list(order) + [extra.astype(BF16)], axis=0)


def tile_kernel(sizes, own_ref, oth_ref, d_ref, w_ref, b_ref, amp_ref, noise_ref, kh_ref, kl_ref, o1h_ref, o1l_ref, o2h_ref, o2l_ref):
    _, npos = sizes
    i, _ = me()
    core0 = (i % 2) == 0
    amp, noise = amp_ref[0], noise_ref[0]
    w_col = w_ref[...]
    own, oth = own_ref[...], oth_ref[...]
    x1 = jnp.where(core0, own, oth)
    x2 = jnp.where(core0, oth, own)
    right1 = features(x1, w_col, False)
    right2 = features(x2, w_col, False)
    mine = features(d_ref[...], w_col, True).astype(F32).T.astype(BF16)
    for right, h_ref, l_ref in ((right1, o1h_ref, o1l_ref), (right2, o2h_ref, o2l_ref)):
        hi, lo = split2(amp * jnp.exp(mm(mine, right)))
        h_ref[...] = hi
        l_ref[...] = lo
    left2 = features(x2, w_col, True).astype(F32).T.astype(BF16)
    b1 = b_ref[0:1, :]
    step = 128
    for r in range(npos // step):
        rows = slice(r * step, (r + 1) * step)
        b2 = jnp.broadcast_to(b_ref[1:2, rows], (step, step)).T[:, :1]
        tile = amp * jnp.exp(mm(left2[rows], right1)) + jnp.where(b2 == b1, noise, 0.0)
        hi, lo = split2(tile)
        kh_ref[rows, :] = hi
        kl_ref[rows, :] = lo


def solve_kernel(sizes, *refs):
    zsize, panel, half = sizes
    u_refs = refs[:zsize]
    kh_ref, kl_ref, a2_ref = refs[zsize : zsize + 3]
    v_refs, o_ref, uu = refs[zsize + 3 : -2], refs[-2], refs[-1]
    _, g = me()
    for s in range(zsize):
        x = u_refs[s][...]
        x = jnp.concatenate([x[:, :half], x[:, half:]], axis=0)
        hi, lo = split2(x)
        at = pl.multiple_of(jnp.bitwise_xor(g, s) * panel, panel)
        uu[pl.ds(at, panel), :] = jnp.concatenate([hi, lo], axis=1)
    y = mm(kh_ref[...], uu[...])
    w = y[:, :half] + y[:, half:] + mm(kl_ref[...], uu[...])[:, :half]
    hi, lo = split2(w)
    y = mm(a2_ref[...], jnp.concatenate([hi, lo], axis=1))
    y = y[:panel, :half] + y[:panel, half:] + y[panel:, :half]
    v = v_refs[0][...]
    for r in v_refs[1:]:
        v = v + r[...]
    o_ref[...] = v - fold(y)


def apply_kernel(sizes, r_ref, x_ref, kh_ref, kl_ref, st_ref, own_ref, oth_ref, noise_ref, ro_ref, xo_ref, uu):
    zsize, panel, half = sizes
    i, g = me()
    core0 = (i % 2) == 0
    noise = noise_ref[0]
    width = 2 * half
    hp = panel // 2
    for s in range(zsize):
        own = own_ref[s * hp : (s + 1) * hp, :]
        oth = oth_ref[s * hp : (s + 1) * hp, :]
        low = jnp.where(core0, own, oth)
        high = jnp.where(core0, oth, own)
        x = jnp.concatenate(
            [
                jnp.concatenate([low[:, :half], high[:, :half]], axis=1),
                jnp.concatenate([low[:, half:], high[:, half:]], axis=1),
            ],
            axis=0,
        )
        hi, lo = split2(x)
        at = pl.multiple_of(jnp.bitwise_xor(g, s) * panel, panel)
        uu[pl.ds(at, panel), :] = jnp.concatenate([hi, lo], axis=1)
    u = uu[...]
    wide = mm(kh_ref[...], u)
    kernel_sum = wide[:, :width] + wide[:, width:] + mm(kl_ref[...], u[:, :width])
    wide = mm(st_ref[...], u)
    inc = wide[:, :width] + wide[:, width:]
    ro_ref[...] = r_ref[...] - kernel_sum - noise * inc
    xo_ref[...] = x_ref[...] + inc


def call(kernel, out_shape, n_in, flops, nbytes, scratch=(), smem_at=()):
    specs = [SMEM if k in smem_at else VMEM for k in range(n_in)]
    return pl.pallas_call(
        kernel,
        out_shape=out_shape,
        in_specs=specs,
        out_specs=jax.tree.map(lambda _: VMEM, out_shape),
        scratch_shapes=list(scratch),
        compiler_params=pltpu.CompilerParams(vmem_limit_bytes=40 << 20),
        cost_estimate=pl.CostEstimate(flops=flops, bytes_accessed=nbytes, transcendentals=0),
    )


def sds(shape, dtype):
    return jax.ShapeDtypeStruct(shape, dtype)


def local(residual_in, solution_in, descriptors, length_weights, amplitude, noise, block_inverse, block_rows):
    rows_local, width = residual_in.shape
    feats = descriptors.shape[0]
    steps, npos = block_rows.shape
    assert steps == 2
    zsize, rsize = lax.axis_size("grp"), lax.axis_size("rows")
    panel = npos // zsize
    half = width // 2
    line = zsize * rows_local

    def over_z(x, s):
        return lax.ppermute(x, "grp", [(k, k ^ s) for k in range(zsize)])

    def over_rows(x, s):
        return lax.ppermute(x, "rows", [(k, k ^ s) for k in range(rsize)])

    def all_z(x):
        return [x] + [over_z(x, s) for s in range(1, zsize)]

    def all_plane(x):
        return [x] + [over_rows(x, s) for s in range(2, rsize, 2)]

    pts_raw = all_z(descriptors)
    raw = all_z(residual_in)

    st, st1, st2 = call(
        functools.partial(select_kernel, (rows_local, zsize)),
        (sds((2, line, npos), BF16), sds((rows_local, npos), BF16), sds((rows_local, npos), BF16)),
        1,
        2 * line * npos,
        5 << 20,
    )(block_rows)
    send, keep = call(
        functools.partial(points_kernel, (rows_local, zsize, feats)),
        (sds((feats, npos), F32),) * 2,
        zsize + 1,
        2 * 2 * 3 * feats * line * npos,
        5 << 20,
    )(*pts_raw, st)
    got = over_rows(send, 1)
    pair = call(add_kernel, sds(keep.shape, F32), 2, keep.size, 12 * keep.size)(keep, got)
    plane = all_plane(pair)
    points = call(sum_kernel, sds(keep.shape, F32), len(plane), keep.size, 16 * keep.size)(*plane)
    points_oth = over_rows(points, 1)

    ah, al, a2 = call(
        functools.partial(columns_kernel, panel),
        (sds((2, panel, line), BF16), sds((2, panel, line), BF16), sds((2 * panel, npos), BF16)),
        2,
        2 * 2 * 2 * panel * line * npos,
        8 << 20,
    )(block_inverse, st)

    send, keep = call(
        functools.partial(part_kernel, (rows_local, zsize, panel)),
        (sds((panel, width), F32),) * 2,
        zsize + 2,
        2 * 2 * panel * line * width * 3,
        4 << 20,
        scratch=[pltpu.VMEM((line, 2 * width), BF16)],
    )(*raw, ah, al)
    got = over_rows(send, 1)
    u_part, v_part = call(pair_kernel, (sds((panel // 2, width), F32),) * 2, 2, keep.size, 12 * keep.size)(keep, got)
    plane = all_plane(u_part)
    u1 = call(sum_kernel, sds(u_part.shape, F32), len(plane), u_part.size, 16 * u_part.size)(*plane)
    u1, v_part = lax.optimization_barrier((u1, v_part))
    u1_all = all_z(u1)
    v2_all = all_plane(v_part)

    kh, kl, o1h, o1l, o2h, o2l = call(
        functools.partial(tile_kernel, (feats, npos)),
        (sds((npos, npos), BF16),) * 2 + (sds((rows_local, npos), BF16),) * 4,
        7,
        2 * npos * npos * 256,
        8 << 20,
        smem_at=(5, 6),
    )(points, points_oth, descriptors, length_weights[:, None], block_rows, amplitude, noise)

    u2 = call(
        functools.partial(solve_kernel, (zsize, panel, half)),
        sds((panel // 2, width), F32),
        zsize + 3 + len(v2_all),
        2 * npos * npos * width * 2,
        6 << 20,
        scratch=[pltpu.VMEM((npos, width), BF16)],
    )(*u1_all, kh, kl, a2, *v2_all)
    u2_all = all_z(u2)

    finish = call(
        functools.partial(apply_kernel, (zsize, panel, half)),
        (sds(residual_in.shape, F32),) * 2,
        8,
        2 * rows_local * npos * width * 5,
        4 << 20,
        scratch=[pltpu.VMEM((npos, 2 * width), BF16)],
        smem_at=(7,),
    )
    own1 = jnp.concatenate(u1_all, axis=0)
    oth1 = over_rows(own1, 1)
    residual, sol = finish(residual_in, solution_in, o1h, o1l, st1, own1, oth1, noise)
    own2 = jnp.concatenate(u2_all, axis=0)
    oth2 = over_rows(own2, 1)
    residual, sol = finish(residual, sol, o2h, o2l, st2, own2, oth2, noise)
    return sol, residual


def solution(mesh):
    both = P(("rows", "grp"), None)

    return jax.shard_map(
        local,
        mesh=mesh,
        in_specs=(both, both, P(None, ("rows", "grp")), P(), P(), P(), P(None, "grp", None), P()),
        out_specs=(both, both),
        check_vma=False,
    )
```

```python
import functools

import jax
import jax.numpy as jnp
from jax import lax
from jax.experimental import pallas as pl
from jax.experimental.pallas import tpu as pltpu
from jax.sharding import PartitionSpec as P


F32 = jnp.float32
BF16 = jnp.bfloat16
LANES = 128
VMEM = pl.BlockSpec(memory_space=pltpu.VMEM)
ANY = pl.BlockSpec(memory_space=pltpu.HBM)
SMEM = pl.BlockSpec(memory_space=pltpu.SMEM)


def split2(x):
    hi = x.astype(BF16)
    return hi, (x - hi.astype(F32)).astype(BF16)


def split3(x):
    hi = x.astype(BF16)
    rest = x - hi.astype(F32)
    mid = rest.astype(BF16)
    return hi, mid, (rest - mid.astype(F32)).astype(BF16)


def mm(a, b):
    return lax.dot_general(a, b, (((1,), (0,)), ((), ())), preferred_element_type=F32)


def mm_nt(a, b):
    return lax.dot_general(a, b, (((1,), (1,)), ((), ())), preferred_element_type=F32)


def me():
    return lax.axis_index("rows"), lax.axis_index("grp")


def origin(g, s, zsize):
    return lax.rem(g + (zsize - s), zsize)


def select_kernel(sizes, b_ref, d_ref, st_ref, own1_ref, own2_ref, do_ref):
    rows_local, zsize = sizes
    i, g = me()
    npos = b_ref.shape[1]
    do_ref[...] = d_ref[...]
    row = lax.broadcasted_iota(jnp.int32, (rows_local, npos), 0)
    for t in range(2):
        for s in range(zsize):
            base = (i * zsize + origin(g, s, zsize)) * rows_local
            sel = jnp.where(row == b_ref[t : t + 1, :] - base, 1.0, 0.0).astype(BF16)
            st_ref[t, s * rows_local : (s + 1) * rows_local, :] = sel
            if s == 0:
                (own1_ref, own2_ref)[t][...] = sel


def columns_kernel(panel, a_ref, st_ref, ah_ref, al_ref, a2_ref):
    for t in range(2):
        hi, lo = split2(a_ref[t])
        both = jnp.concatenate([hi, lo], axis=0)
        if t == 1:
            a2_ref[...] = both
        out = mm_nt(both, st_ref[t]).astype(BF16)
        ah_ref[t] = out[:panel]
        al_ref[t] = out[panel:]


def fold(x):
    n = x.shape[0] // 2
    return jnp.concatenate([x[:n], x[n:]], axis=1)


def points_kernel(sizes, *refs):
    zsize, feats = sizes
    d_refs = refs[:zsize]
    st_ref, send_ref, keep_ref = refs[zsize:]
    i, _ = me()
    core0 = (i % 2) == 0
    d = jnp.concatenate([r[...] for r in d_refs], axis=1)
    d3 = jnp.concatenate(list(split3(d)), axis=0)
    points = []
    for t in range(2):
        three = mm(d3, st_ref[t])
        points.append(three[:feats] + three[feats : 2 * feats] + three[2 * feats :])
    keep_ref[...] = jnp.where(core0, points[0], points[1])
    send_ref[...] = jnp.where(core0, points[1], points[0])


def part_kernel(sizes, *refs):
    rows_local, zsize, panel = sizes
    x_refs = refs[:zsize]
    ah_ref, al_ref, send_ref, keep_ref, rr = refs[zsize:]
    i, _ = me()
    core0 = (i % 2) == 0
    width = x_refs[0].shape[1]
    half = width // 2
    hp = panel // 2
    for s in range(zsize):
        hi, lo = split2(x_refs[s][...])
        rr[s * rows_local : (s + 1) * rows_local, :width] = hi
        rr[s * rows_local : (s + 1) * rows_local, width:] = lo
    for t in range(2):
        wide = mm(ah_ref[t], rr[...])
        part = wide[:, :width] + wide[:, width:] + mm(al_ref[t], rr[:, :width])
        low, high = fold(part[:, :half]), fold(part[:, half:])
        keep_ref[t * hp : (t + 1) * hp, :] = jnp.where(core0, low, high)
        send_ref[t * hp : (t + 1) * hp, :] = jnp.where(core0, high, low)


def add_kernel(a_ref, b_ref, o_ref):
    o_ref[...] = a_ref[...] + b_ref[...]


def sum_kernel(count, *refs):
    at = 0
    for out in refs[count:]:
        n = out.shape[0]
        total = refs[0][at : at + n, :]
        for r in refs[1:count]:
            total = total + r[at : at + n, :]
        out[...] = total
        at += n


def features(x, w_col, left):
    weighted = x * w_col
    sq = jnp.sum(weighted * x, axis=0, keepdims=True)
    n = x.shape[1]
    row = lax.broadcasted_iota(jnp.int32, (16, n), 0)
    s0, s1, s2 = (p.astype(F32) for p in split3(sq))
    one = jnp.ones((1, n), F32)
    if left:
        a, b, c = split3(2.0 * weighted)
        extra = jnp.where(row == 0, s0, jnp.where(row == 1, s1, jnp.where(row == 2, s2, 0.0)))
        extra = jnp.where((row >= 3) & (row < 6), 1.0, extra)
        order = (a, a, b, b, a, c)
    else:
        a, b, c = split3(x)
        extra = jnp.where(row == 3, -s0, jnp.where(row == 4, -s1, jnp.where(row == 5, -s2, 0.0)))
        extra = jnp.where(row < 3, -1.0, extra)
        order = (a, b, a, b, c, a)
    return jnp.concatenate(list(order) + [extra.astype(BF16)], axis=0)


def mix_kernel(npos, own_ref, oth_ref, w_ref, b_ref, amp_ref, noise_ref, a2_ref, m_ref, acc):
    i, _ = me()
    core0 = (i % 2) == 0
    panel = acc.shape[0]
    amp, noise = amp_ref[0], noise_ref[0]
    w_col = w_ref[...]
    own, oth = own_ref[...], oth_ref[...]
    right = features(jnp.where(core0, own, oth), w_col, False)
    left = features(jnp.where(core0, oth, own), w_col, True).astype(F32).T.astype(BF16)
    b1 = b_ref[0:1, :]
    step = 256
    for r in range(npos // step):
        rows = slice(r * step, (r + 1) * step)
        b2 = jnp.broadcast_to(b_ref[1:2, rows], (LANES, step)).T[:, :1]
        tile = amp * jnp.exp(mm(left[rows], right)) + jnp.where(b2 == b1, noise, 0.0)
        hi, lo = split2(tile)
        wide = mm(a2_ref[:, rows], hi)
        part = wide[:panel] + wide[panel:] + mm(a2_ref[:panel, rows], lo)
        if r == 0:
            acc[...] = part
        else:
            acc[...] += part
    hi, lo = split2(acc[...])
    m_ref[:panel, :] = hi
    m_ref[panel:, :] = lo


def own_kernel(own_ref, oth_ref, d_ref, w_ref, amp_ref, o1h_ref, o1l_ref, o2h_ref, o2l_ref):
    i, _ = me()
    core0 = (i % 2) == 0
    w_col = w_ref[...]
    own, oth = own_ref[...], oth_ref[...]
    mine = features(d_ref[...], w_col, True).astype(F32).T.astype(BF16)
    x1, x2 = jnp.where(core0, own, oth), jnp.where(core0, oth, own)
    for x, h_ref, l_ref in ((x1, o1h_ref, o1l_ref), (x2, o2h_ref, o2l_ref)):
        hi, lo = split2(amp_ref[0] * jnp.exp(mm(mine, features(x, w_col, False))))
        h_ref[...] = hi
        l_ref[...] = lo


def solve_kernel(sizes, *refs):
    zsize, panel, half = sizes
    u_refs = refs[:zsize]
    v_ref, m_ref, o_ref, uu = refs[zsize:]
    _, g = me()
    for s in range(zsize):
        x = u_refs[s][...]
        x = jnp.concatenate([x[:, :half], x[:, half:]], axis=0)
        hi, lo = split2(x)
        at = pl.multiple_of(origin(g, s, zsize) * panel, panel)
        uu[pl.ds(at, panel), :] = jnp.concatenate([hi, lo], axis=1)
    y = mm(m_ref[...], uu[...])
    y = y[:panel, :half] + y[:panel, half:] + y[panel:, :half]
    o_ref[...] = v_ref[...] - fold(y)


def apply_kernel(sizes, r_ref, x_ref, kh_ref, kl_ref, st_ref, own_ref, oth_ref, noise_ref, ro_ref, xo_ref, uu):
    zsize, panel, half = sizes
    i, g = me()
    core0 = (i % 2) == 0
    noise = noise_ref[0]
    width = 2 * half
    hp = panel // 2
    for s in range(zsize):
        own = own_ref[s * hp : (s + 1) * hp, :]
        oth = oth_ref[s * hp : (s + 1) * hp, :]
        low = jnp.where(core0, own, oth)
        high = jnp.where(core0, oth, own)
        x = jnp.concatenate(
            [
                jnp.concatenate([low[:, :half], high[:, :half]], axis=1),
                jnp.concatenate([low[:, half:], high[:, half:]], axis=1),
            ],
            axis=0,
        )
        hi, lo = split2(x)
        at = pl.multiple_of(origin(g, s, zsize) * panel, panel)
        uu[pl.ds(at, panel), :] = jnp.concatenate([hi, lo], axis=1)
    u = uu[...]
    wide = mm(kh_ref[...], u)
    kernel_sum = wide[:, :width] + wide[:, width:] + mm(kl_ref[...], u[:, :width])
    wide = mm(st_ref[...], u)
    inc = wide[:, :width] + wide[:, width:]
    ro_ref[...] = r_ref[...] - kernel_sum - noise * inc
    xo_ref[...] = x_ref[...] + inc


def call(kernel, out_shape, n_in, flops, nbytes, scratch=(), smem_at=(), any_at=()):
    specs = [SMEM if k in smem_at else ANY if k in any_at else VMEM for k in range(n_in)]
    return pl.pallas_call(
        kernel,
        out_shape=out_shape,
        in_specs=specs,
        out_specs=jax.tree.map(lambda _: VMEM, out_shape),
        scratch_shapes=list(scratch),
        compiler_params=pltpu.CompilerParams(vmem_limit_bytes=40 << 20),
        cost_estimate=pl.CostEstimate(flops=flops, bytes_accessed=nbytes, transcendentals=0),
    )


def sds(shape, dtype):
    return jax.ShapeDtypeStruct(shape, dtype)


def local(residual_in, solution_in, descriptors, length_weights, amplitude, noise, block_inverse, block_rows):
    rows_local, width = residual_in.shape
    feats = descriptors.shape[0]
    steps, npos = block_rows.shape
    assert steps == 2
    zsize, rsize = lax.axis_size("grp"), lax.axis_size("rows")
    panel = npos // zsize
    half = width // 2
    line = zsize * rows_local

    def over_rows(x, s):
        return lax.ppermute(x, "rows", [(k, k ^ s) for k in range(rsize)])

    def all_z(x):
        return [x] + [
            lax.ppermute(x, "grp", [(k, (k + s) % zsize) for k in range(zsize)]) for s in range(1, zsize)
        ]

    def all_plane(x):
        return [x] + [over_rows(x, s) for s in range(2, rsize, 2)]

    def plus(a, b):
        return call(add_kernel, sds(a.shape, F32), 2, a.size, 12 * a.size)(a, b)

    pts_raw = all_z(descriptors)
    raw = all_z(residual_in)

    own = sds((rows_local, npos), BF16)
    st, st1, st2, mine = call(
        functools.partial(select_kernel, (rows_local, zsize)),
        (sds((2, line, npos), BF16), own, own, sds(descriptors.shape, F32)),
        2,
        2 * line * npos,
        5 << 20,
    )(block_rows, descriptors)
    ah, al, a2 = call(
        functools.partial(columns_kernel, panel),
        (sds((2, panel, line), BF16), sds((2, panel, line), BF16), sds((2 * panel, npos), BF16)),
        2,
        2 * 2 * 2 * panel * line * npos,
        8 << 20,
    )(block_inverse, st)

    send, points = call(
        functools.partial(points_kernel, (zsize, feats)),
        (sds((feats, npos), F32),) * 2,
        zsize + 1,
        2 * 2 * 3 * feats * line * npos,
        5 << 20,
    )(mine, *pts_raw[1:], st)
    got = over_rows(send, 1)
    points = plus(points, got)
    s = 2
    while s < rsize:
        got = over_rows(points, s)
        points = plus(points, got)
        s *= 2
    points_oth = over_rows(points, 1)

    send, keep = call(
        functools.partial(part_kernel, (rows_local, zsize, panel)),
        (sds((panel, width), F32),) * 2,
        zsize + 2,
        2 * 2 * panel * line * width * 3,
        4 << 20,
        scratch=[pltpu.VMEM((line, 2 * width), BF16)],
    )(*raw, ah, al)
    got = over_rows(send, 1)
    hp = panel // 2
    pair = plus(keep, got)
    plane = all_plane(pair)
    u1, v2 = call(
        functools.partial(sum_kernel, len(plane)), (sds((hp, width), F32),) * 2, len(plane), pair.size, 1 << 19
    )(*plane)
    u1_all = all_z(u1)

    w_col = length_weights[:, None]
    mixed = call(
        functools.partial(mix_kernel, npos),
        sds((2 * panel, npos), BF16),
        7,
        2 * npos * npos * (256 + 3 * panel),
        3 << 20,
        scratch=[pltpu.VMEM((panel, npos), F32)],
        smem_at=(4, 5),
    )(points, points_oth, w_col, block_rows, amplitude, noise, a2)
    o1h, o1l, o2h, o2l = call(
        own_kernel,
        (sds((rows_local, npos), BF16),) * 4,
        5,
        4 * rows_local * npos * 256,
        3 << 20,
        smem_at=(4,),
    )(points, points_oth, mine, w_col, amplitude)

    u2 = call(
        functools.partial(solve_kernel, (zsize, panel, half)),
        sds((hp, width), F32),
        zsize + 2,
        4 * panel * npos * width,
        2 << 20,
        scratch=[pltpu.VMEM((npos, width), BF16)],
    )(*u1_all, v2, mixed)
    u2_all = all_z(u2)

    finish = call(
        functools.partial(apply_kernel, (zsize, panel, half)),
        (sds(residual_in.shape, F32),) * 2,
        8,
        2 * rows_local * npos * width * 5,
        4 << 20,
        scratch=[pltpu.VMEM((npos, 2 * width), BF16)],
        smem_at=(7,),
    )
    own1 = jnp.concatenate(u1_all, axis=0)
    oth1 = over_rows(own1, 1)
    residual, sol = finish(residual_in, solution_in, o1h, o1l, st1, own1, oth1, noise)
    own2 = jnp.concatenate(u2_all, axis=0)
    oth2 = over_rows(own2, 1)
    residual, sol = finish(residual, sol, o2h, o2l, st2, own2, oth2, noise)
    return sol, residual


def solution(mesh):
    both = P(("rows", "grp"), None)

    return jax.shard_map(
        local,
        mesh=mesh,
        in_specs=(both, both, P(None, ("rows", "grp")), P(), P(), P(), P(None, "grp", None), P()),
        out_specs=(both, both),
        check_vma=False,
    )
```
